32 devices in a mesh: inp: 4 (over y, core), hid: 8 (over z, x).
Axes of the slice: x: 2, y: 2, z: 4, core: 2. Of those that a mesh axis runs over, the one named last changes fastest.
Arguments:
- inputs: bfloat16 [128, 16384], P(None, 'inp'), may hold values from -6 to 6
- out_grad: bfloat16 [128, 16384], P(None, 'inp'), may hold values from -6 to 6
- gate_index: int32 [8192, 26624], P('inp', 'hid'), may hold values from 0 to 255, as said below
- up_index: int32 [8192, 26624], P('inp', 'hid'), may hold values from 0 to 255, as said below
- down_index: int32 [13312, 16384], P('hid', 'inp'), may hold values from 0 to 255, as said below
- gate_table: float32 [16, 26624], P(None, 'hid'), may hold values from -0.046875 to 0.046875
- up_table: float32 [16, 26624], P(None, 'hid'), may hold values from -0.046875 to 0.046875
- down_table: float32 [16, 16384], P(None, 'inp'), may hold values from -0.0390625 to 0.0390625
Outputs:
- input_grad: bfloat16 [128, 16384], P('hid', 'inp')
- gate_table_grad: float32 [16, 26624], P(None, 'hid')
- up_table_grad: float32 [16, 26624], P(None, 'hid')
- down_table_grad: float32 [16, 16384], P(None, 'inp')
The draws below stay inside these ranges and needn't reach their ends.
Inputs may be any that keep to these rules, and one draw needn't show every extreme that they name: `gate_index`: each word holds two independent 4-bit table entries. `up_index`: each word holds two independent 4-bit table entries. `down_index`: each word holds two independent 4-bit table entries.
All inputs are finite; a program needn't handle non-finite values.
Results may differ from the reference program's by a relative error of at most 0.0072.
Values may be sent and summed in bfloat16 or wider, within the bound.
A program may use at most 512 MiB of HBM per device.

```python
import jax
import jax.numpy as jnp
from jax import lax

D = 16384
FF = 26624
ENTRIES = 16
TOKENS = 128
N_HID = 8


def packed_words(key, salt, rows, cols):
    sub = jax.random.fold_in(key, salt)
    words = jax.random.randint(sub, (rows, cols), 0, 256, dtype=jnp.int32)
    return words.at[0, 0].set(255).at[0, 1].set(0)


def draw_gate_index(key, part):
    return packed_words(key, 7101, D // 2, FF)


def draw_up_index(key, part):
    return packed_words(key, 7202, D // 2, FF)


def draw_down_index(key, part):
    return packed_words(key, 7303, FF // 2, D)


def levels(rng, shape, split, low, high):
    def one(dim, blocks):
        steps = jax.random.uniform(jax.random.fold_in(jax.random.fold_in(rng, 6), dim), (blocks,), jnp.float32, low / len(split), high / len(split))
        return jnp.repeat(jnp.exp(steps), shape[dim] // blocks).reshape((-1,) + (1,) * (len(shape) - dim - 1))

    gain = one(*split[0])
    for cut in split[1:]:
        gain = gain * one(*cut)
    return gain


def gaussian(stream_key, extent, scale, most, split=(), held_as=jnp.bfloat16):
    values = jax.random.normal(stream_key, extent, jnp.float32) * scale
    if len(split) > 0:
        values = levels(stream_key, extent, split, -0.22, 0.18) * values
    return jnp.clip(values, min=-most, max=most).astype(held_as)


def setup_inputs(seed: int = 0) -> dict:
    key_of = jax.random.split(jax.random.key(seed), 9)
    inputs = gaussian(key_of[0], (TOKENS, D), 1.0, 6.0, ((1, 4),))
    out_grad = gaussian(key_of[1], (TOKENS, D), 1.0, 6.0, ((1, 4),))
    gate_index = draw_gate_index(jax.random.fold_in(key_of[8], 71), 0)
    up_index = draw_up_index(jax.random.fold_in(key_of[8], 71), 0)
    down_index = draw_down_index(jax.random.fold_in(key_of[8], 71), 0)
    gate_table = gaussian(key_of[5], (ENTRIES, FF), D ** -0.5, 0.046875, ((1, 8),), jnp.float32)
    up_table = gaussian(key_of[6], (ENTRIES, FF), D ** -0.5, 0.046875, ((1, 8),), jnp.float32)
    down_table = gaussian(key_of[7], (ENTRIES, D), FF ** -0.5, 0.0390625, ((1, 4),), jnp.float32)
    return {"inputs": inputs, "out_grad": out_grad, "gate_index": gate_index, "up_index": up_index, "down_index": down_index, "gate_table": gate_table, "up_table": up_table, "down_table": down_table}


def unpack(packed):
    parts = [jnp.bitwise_and(jnp.right_shift(packed, 4 * nibble), 15) for nibble in range(2)]
    stacked = jnp.stack(parts, axis=1)
    return stacked.reshape(packed.shape[0] * 2, packed.shape[1]).astype(jnp.int32)


def decode(indices, lookup):
    summed = jnp.zeros(indices.shape, jnp.float32)
    for bucket in range(16):
        summed = summed + jnp.where(indices == bucket, lookup[bucket][None, :], 0.0)
    return summed.astype(jnp.bfloat16)


def binned(grads, indices):
    return jnp.stack([jnp.sum(jnp.where(indices == bucket, grads, 0.0), axis=0) for bucket in range(16)])


def reference(inputs, out_grad, gate_index, up_index, down_index, gate_table, up_table, down_table):
    blocks = N_HID
    block_width = FF // blocks
    scale = 1.0 / TOKENS

    def one_block(carry, block_id):
        input_acc, down_acc = carry
        begin = (block_id * block_width).astype(jnp.int32)
        packed_begin = (block_id * (block_width // 2)).astype(jnp.int32)
        idx_gate = unpack(lax.dynamic_slice_in_dim(gate_index, begin, block_width, 1))
        idx_up = unpack(lax.dynamic_slice_in_dim(up_index, begin, block_width, 1))
        idx_down = unpack(lax.dynamic_slice_in_dim(down_index, packed_begin, block_width // 2, 0))
        w_gate = decode(idx_gate, lax.dynamic_slice_in_dim(gate_table, begin, block_width, 1))
        w_up = decode(idx_up, lax.dynamic_slice_in_dim(up_table, begin, block_width, 1))
        w_down = decode(idx_down, down_table)
        pre_gate = jnp.dot(inputs, w_gate, preferred_element_type=jnp.float32)
        pre_up = jnp.dot(inputs, w_up, preferred_element_type=jnp.float32)
        hidden_grad = jnp.dot(out_grad, w_down.T, preferred_element_type=jnp.float32)
        sig_gate = jax.nn.sigmoid(pre_gate)
        silu_gate = pre_gate * sig_gate
        activ = (silu_gate * pre_up).astype(jnp.bfloat16)
        gate_grad = (hidden_grad * pre_up * sig_gate * (1.0 + pre_gate * (1.0 - sig_gate))).astype(jnp.bfloat16)
        up_grad = (hidden_grad * silu_gate).astype(jnp.bfloat16)
        input_acc = input_acc + jnp.dot(gate_grad, w_gate.T, preferred_element_type=jnp.float32) + jnp.dot(up_grad, w_up.T, preferred_element_type=jnp.float32)
        gate_bins = binned(jnp.dot(inputs.T, gate_grad, preferred_element_type=jnp.float32), idx_gate) * scale
        up_bins = binned(jnp.dot(inputs.T, up_grad, preferred_element_type=jnp.float32), idx_up) * scale
        down_acc = down_acc + binned(jnp.dot(activ.T, out_grad, preferred_element_type=jnp.float32), idx_down)
        return (input_acc, down_acc), (gate_bins, up_bins)

    start_carry = (jnp.zeros((TOKENS, D), jnp.float32), jnp.zeros((16, D), jnp.float32))
    (input_acc, down_acc), (gate_bins, up_bins) = lax.scan(one_block, start_carry, jnp.arange(blocks, dtype=jnp.int32))
    gate_table_grad = jnp.transpose(gate_bins, (1, 0, 2)).reshape(16, FF)
    up_table_grad = jnp.transpose(up_bins, (1, 0, 2)).reshape(16, FF)
    return input_acc.astype(jnp.bfloat16), gate_table_grad, up_table_grad, down_acc * scale
```

```python
import functools
import math

import jax
import jax.numpy as jnp
from jax import lax
from jax.experimental import pallas as pl
from jax.experimental.pallas import tpu as pltpu
from jax.sharding import PartitionSpec as P

LANES = 128
SUB = 16
F32 = jnp.float32
BF16 = jnp.bfloat16


def divisor(size, most, unit=LANES):
    best = unit
    for cand in range(unit, most + 1, unit):
        if size % cand == 0:
            best = cand
    return best


def bit_masks(words, parity):
    return [(words & jnp.int16(1 << (4 * parity + bit))) != 0 for bit in range(4)]


def look_up(levels, masks):
    for mask in masks:
        levels = [jnp.where(mask, levels[i + 1], levels[i]) for i in range(0, len(levels), 2)]
    return levels[0]


def table_rows(table_ref, lanes):
    return [
        jnp.broadcast_to(table_ref[k : k + 1, lanes], (SUB, LANES)).astype(BF16)
        for k in range(16)
    ]


def decode_block(idx_ref, table, lanes, start, count, even_ref, odd_ref, base):
    for step in range(count // SUB):
        row = start + step * SUB
        words = idx_ref[pl.ds(row, SUB), lanes].astype(jnp.int16)
        dst = pl.ds(base + step * SUB, SUB)
        even_ref[dst, lanes] = look_up(table, bit_masks(words, 0))
        odd_ref[dst, lanes] = look_up(table, bit_masks(words, 1))


def up_kernel(block, xe_ref, xo_ref, gi_ref, ui_ref, gt_ref, ut_ref, pg_ref, pu_ref, ge_ref, go_ref, ue_ref, uo_ref):
    words, cols = gi_ref.shape
    for idx_ref, table_ref, even_ref, odd_ref, out_ref in (
        (gi_ref, gt_ref, ge_ref, go_ref, pg_ref),
        (ui_ref, ut_ref, ue_ref, uo_ref, pu_ref),
    ):
        for chunk in range(cols // LANES):
            lanes = slice(chunk * LANES, (chunk + 1) * LANES)
            table = table_rows(table_ref, lanes)

            def body(i, carry):
                start = pl.multiple_of(i * block, block)
                decode_block(idx_ref, table, lanes, start, block, even_ref, odd_ref, start)
                return carry

            lax.fori_loop(0, words // block, body, 0)
        out_ref[...] = jnp.dot(xe_ref[...], even_ref[...], preferred_element_type=F32) + jnp.dot(
            xo_ref[...], odd_ref[...], preferred_element_type=F32
        )


def up_products(x_even, x_odd, gate_index, up_index, gate_table, up_table):
    tokens = x_even.shape[0]
    words, width = gate_index.shape
    cols = divisor(width, 256)
    block = math.gcd(words, 128)
    whole = pl.BlockSpec((tokens, words), lambda j: (0, 0))
    tile = pl.BlockSpec((words, cols), lambda j: (0, j))
    lut = pl.BlockSpec((16, cols), lambda j: (0, j))
    pre = pl.BlockSpec((tokens, cols), lambda j: (0, j))
    weight = jax.ShapeDtypeStruct((words, width), BF16)
    return pl.pallas_call(
        functools.partial(up_kernel, block),
        grid=(width // cols,),
        in_specs=[whole, whole, tile, tile, lut, lut],
        out_specs=[pre, pre, tile, tile, tile, tile],
        out_shape=[jax.ShapeDtypeStruct((tokens, width), F32)] * 2 + [weight] * 4,
        name="up_products",
    )(x_even, x_odd, gate_index, up_index, gate_table, up_table)


def contract_cols(left, right):
    return lax.dot_general(left, right, (((1,), (1,)), ((), ())), preferred_element_type=F32)


def down_kernel(block, og_ref, di_ref, dt_ref, he_ref, ho_ref, even_ref, odd_ref):
    words, cols = di_ref.shape

    @pl.when(pl.program_id(0) == 0)
    def _():
        he_ref[...] = jnp.zeros_like(he_ref)
        ho_ref[...] = jnp.zeros_like(ho_ref)

    for chunk in range(cols // LANES):
        lanes = slice(chunk * LANES, (chunk + 1) * LANES)
        table = table_rows(dt_ref, lanes)

        def body(i, carry):
            start = pl.multiple_of(i * block, block)
            decode_block(di_ref, table, lanes, start, block, even_ref, odd_ref, start)
            return carry

        lax.fori_loop(0, words // block, body, 0)
    he_ref[...] += contract_cols(og_ref[...], even_ref[...])
    ho_ref[...] += contract_cols(og_ref[...], odd_ref[...])


def down_products(out_grad, down_index, down_table):
    tokens = out_grad.shape[0]
    words, width = down_index.shape
    cols = divisor(width, 256)
    block = math.gcd(words, 128)
    whole = pl.BlockSpec((tokens, words), lambda j: (0, 0))
    return pl.pallas_call(
        functools.partial(down_kernel, block),
        grid=(width // cols,),
        in_specs=[
            pl.BlockSpec((tokens, cols), lambda j: (0, j)),
            pl.BlockSpec((words, cols), lambda j: (0, j)),
            pl.BlockSpec((16, cols), lambda j: (0, j)),
        ],
        out_specs=[whole, whole],
        out_shape=[jax.ShapeDtypeStruct((tokens, words), F32)] * 2,
        scratch_shapes=[pltpu.VMEM((words, cols), BF16)] * 2,
        name="down_products",
    )(out_grad, down_index, down_table)


def leaves(value, masks):
    b0, b1, b2, b3 = masks
    zero = jnp.zeros_like(value)
    out = []
    for part in (jnp.where(b3, zero, value), jnp.where(b3, value, zero)):
        for piece in (jnp.where(b2, zero, part), jnp.where(b2, part, zero)):
            one = jnp.where(b1, piece, zero)
            out += [piece, jnp.where(b0, piece, zero), one, jnp.where(b0, one, zero)]
    return out


def bin_block(idx_ref, lanes, start, count, even_ref, odd_ref, acc_ref):
    sums = None
    for step in range(count // SUB):
        words = idx_ref[pl.ds(start + step * SUB, SUB), lanes].astype(jnp.int16)
        for parity, ref in ((0, even_ref), (1, odd_ref)):
            value = ref[step * SUB : (step + 1) * SUB, lanes].astype(BF16)
            parts = leaves(value, bit_masks(words, parity))
            sums = parts if sums is None else [a + b for a, b in zip(sums, parts)]
    for k, total in enumerate(sums):
        wide = total.astype(F32)
        acc_ref[8 * k : 8 * k + 8, lanes] += wide[:8] + wide[8:]


def write_bins(acc_ref, out_ref, scale):
    rows = [jnp.sum(acc_ref[8 * k : 8 * k + 8, :], axis=0, keepdims=True) for k in range(16)]
    for k in range(0, 16, 4):
        none, low, high, both = rows[k : k + 4]
        out_ref[k : k + 1, :] = ((none - low) - (high - both)) * scale
        out_ref[k + 1 : k + 2, :] = (low - both) * scale
        out_ref[k + 2 : k + 3, :] = (high - both) * scale
        out_ref[k + 3 : k + 4, :] = both * scale


def bin_columns(block, scale, left_even, left_odd, right, idx_ref, out_ref, acc_ref, pe_ref, po_ref):
    words, cols = idx_ref.shape
    acc_ref[...] = jnp.zeros_like(acc_ref)

    def body(i, carry):
        start = pl.multiple_of(i * block, block)
        pe_ref[...] = jnp.dot(left_even[pl.ds(start, block), :], right, preferred_element_type=F32)
        po_ref[...] = jnp.dot(left_odd[pl.ds(start, block), :], right, preferred_element_type=F32)
        for chunk in range(cols // LANES):
            lanes = slice(chunk * LANES, (chunk + 1) * LANES)
            bin_block(idx_ref, lanes, start, block, pe_ref, po_ref, acc_ref)
        return carry

    lax.fori_loop(0, words // block, body, 0)
    write_bins(acc_ref, out_ref, scale)


def back_kernel(block, scale, xe_ref, xo_ref, gg_ref, ug_ref, gi_ref, ui_ref, ge_ref, go_ref, ue_ref, uo_ref,
                de_ref, do_ref, gb_ref, ub_ref, acc_ref, pe_ref, po_ref):
    @pl.when(pl.program_id(0) == 0)
    def _():
        de_ref[...] = jnp.zeros_like(de_ref)
        do_ref[...] = jnp.zeros_like(do_ref)

    gate, up = gg_ref[...], ug_ref[...]
    de_ref[...] += contract_cols(gate, ge_ref[...]) + contract_cols(up, ue_ref[...])
    do_ref[...] += contract_cols(gate, go_ref[...]) + contract_cols(up, uo_ref[...])
    for grad, idx_ref, out_ref in ((gate, gi_ref, gb_ref), (up, ui_ref, ub_ref)):
        bin_columns(block, scale, xe_ref, xo_ref, grad, idx_ref, out_ref, acc_ref, pe_ref, po_ref)


def back_products(x_even, x_odd, gate_grad, up_grad, gate_index, up_index, weights, scale):
    tokens = gate_grad.shape[0]
    words, width = gate_index.shape
    cols = divisor(width, 256)
    block = math.gcd(words, 128)
    rows = pl.BlockSpec((words, tokens), lambda j: (0, 0))
    grad = pl.BlockSpec((tokens, cols), lambda j: (0, j))
    tile = pl.BlockSpec((words, cols), lambda j: (0, j))
    whole = pl.BlockSpec((tokens, words), lambda j: (0, 0))
    bins = pl.BlockSpec((16, cols), lambda j: (0, j))
    return pl.pallas_call(
        functools.partial(back_kernel, block, scale),
        grid=(width // cols,),
        in_specs=[rows, rows, grad, grad] + [tile] * 6,
        out_specs=[whole, whole, bins, bins],
        out_shape=[jax.ShapeDtypeStruct((tokens, words), F32)] * 2
        + [jax.ShapeDtypeStruct((16, width), F32)] * 2,
        scratch_shapes=[pltpu.VMEM((128, cols), F32)] + [pltpu.VMEM((block, cols), F32)] * 2,
        name="back_products",
    )(x_even.T, x_odd.T, gate_grad, up_grad, gate_index, up_index, *weights)


def bins_kernel(block, scale, ae_ref, ao_ref, og_ref, di_ref, out_ref, acc_ref, pe_ref, po_ref):
    bin_columns(block, scale, ae_ref, ao_ref, og_ref[...], di_ref, out_ref, acc_ref, pe_ref, po_ref)


def down_bins(act_even, act_odd, out_grad, down_index, scale):
    tokens = out_grad.shape[0]
    words, width = down_index.shape
    cols = divisor(width, 256)
    block = math.gcd(words, 128)
    rows = pl.BlockSpec((words, tokens), lambda j: (0, 0))
    return pl.pallas_call(
        functools.partial(bins_kernel, block, scale),
        grid=(width // cols,),
        in_specs=[
            rows,
            rows,
            pl.BlockSpec((tokens, cols), lambda j: (0, j)),
            pl.BlockSpec((words, cols), lambda j: (0, j)),
        ],
        out_specs=pl.BlockSpec((16, cols), lambda j: (0, j)),
        out_shape=jax.ShapeDtypeStruct((16, width), F32),
        scratch_shapes=[pltpu.VMEM((128, cols), F32)] + [pltpu.VMEM((block, cols), F32)] * 2,
        name="down_bins",
    )(act_even.T, act_odd.T, out_grad, down_index)


def pairing(block, dtype):
    row = jnp.arange(block)[:, None]
    col = jnp.arange(block)[None, :]
    half = block // 2
    return (row == 2 * (col % half) + col // half).astype(dtype)


def split_pairs(array):
    rows, cols = array.shape
    block = math.gcd(cols, 256)
    out = lax.dot_general(
        array.reshape(rows, cols // block, block), pairing(block, array.dtype), (((2,), (0,)), ((), ())),
        preferred_element_type=F32,
    ).astype(array.dtype)
    half = block // 2
    return out[:, :, :half].reshape(rows, cols // 2), out[:, :, half:].reshape(rows, cols // 2)


def merge_pairs(even, odd):
    rows, cols = even.shape
    block = math.gcd(2 * cols, 256)
    half = block // 2
    both = jnp.concatenate(
        [even.reshape(rows, cols // half, half), odd.reshape(rows, cols // half, half)], axis=2
    )
    return lax.dot_general(
        both, pairing(block, even.dtype), (((2,), (1,)), ((), ())), precision=lax.Precision.HIGHEST,
        preferred_element_type=F32,
    ).reshape(rows, 2 * cols)


def local_hidden(pre_gate, pre_up, hidden_grad):
    sig_gate = jax.nn.sigmoid(pre_gate)
    silu_gate = pre_gate * sig_gate
    activ = (silu_gate * pre_up).astype(BF16)
    gate_grad = (hidden_grad * pre_up * sig_gate * (1.0 + pre_gate * (1.0 - sig_gate))).astype(BF16)
    up_grad = (hidden_grad * silu_gate).astype(BF16)
    return activ, gate_grad, up_grad


def shards(inputs, out_grad, gate_index, up_index, down_index, gate_table, up_table, down_table):
    tokens = inputs.shape[0]
    width = gate_index.shape[1]
    scale = 1.0 / tokens
    x_even, x_odd = split_pairs(inputs)
    pre_gate, pre_up, *weights = up_products(x_even, x_odd, gate_index, up_index, gate_table, up_table)
    share = lax.psum_scatter(
        jnp.concatenate([pre_gate, pre_up], axis=1), "inp", scatter_dimension=0, tiled=True
    )
    hid_even, hid_odd = down_products(out_grad, down_index, down_table)
    hid = lax.psum_scatter(
        jnp.concatenate([hid_even, hid_odd], axis=1), "inp", scatter_dimension=0, tiled=True
    )
    hidden_grad = merge_pairs(hid[:, : width // 2], hid[:, width // 2 :])
    activ, gate_grad, up_grad = local_hidden(share[:, :width], share[:, width:], hidden_grad)
    act_even, act_odd = split_pairs(activ)
    grads = lax.all_gather(jnp.concatenate([gate_grad, up_grad], axis=1), "inp", axis=0, tiled=True)
    acts = lax.all_gather(jnp.concatenate([act_even, act_odd], axis=1), "inp", axis=0, tiled=True)
    din_even, din_odd, gate_bins, up_bins = back_products(
        x_even, x_odd, grads[:, :width], grads[:, width:], gate_index, up_index, weights, scale
    )
    half = din_even.shape[1]
    din = lax.psum_scatter(
        jnp.concatenate([din_even, din_odd], axis=1), "hid", scatter_dimension=0, tiled=True
    )
    input_grad = merge_pairs(din[:, :half], din[:, half:]).astype(BF16)
    gate_sum, up_sum = lax.psum((gate_bins, up_bins), "inp")
    down_sum = lax.psum(
        down_bins(acts[:, : width // 2], acts[:, width // 2 :], out_grad, down_index, scale), "hid"
    )
    return input_grad, gate_sum, up_sum, down_sum


def solution(mesh):
    in_specs = (
        P(None, "inp"),
        P(None, "inp"),
        P("inp", "hid"),
        P("inp", "hid"),
        P("hid", "inp"),
        P(None, "hid"),
        P(None, "hid"),
        P(None, "inp"),
    )
    out_specs = (P("hid", "inp"), P(None, "hid"), P(None, "hid"), P(None, "inp"))
    return jax.shard_map(shards, mesh=mesh, in_specs=in_specs, out_specs=out_specs, check_vma=False)
```

```python
import functools
import math

import jax
import jax.numpy as jnp
from jax import lax
from jax.experimental import pallas as pl
from jax.experimental.pallas import tpu as pltpu
from jax.sharding import PartitionSpec as P

LANES = 128
SUB = 16
F32 = jnp.float32
BF16 = jnp.bfloat16


def divisor(size, most, unit=LANES):
    best = unit
    for cand in range(unit, most + 1, unit):
        if size % cand == 0:
            best = cand
    return best


def bit_masks(words, parity):
    return [(words & jnp.int16(1 << (4 * parity + bit))) != 0 for bit in range(4)]


def look_up(levels, masks):
    for mask in masks:
        levels = [jnp.where(mask, levels[i + 1], levels[i]) for i in range(0, len(levels), 2)]
    return levels[0]


def table_rows(table_ref, lanes):
    return [
        jnp.broadcast_to(table_ref[k : k + 1, lanes], (SUB, LANES)).astype(BF16)
        for k in range(16)
    ]


def pipelined(count, make, use):
    make(0, 0)

    def body(j, carry):
        make(2 * j + 1, 1)
        use(2 * j, 0)
        make(2 * j + 2, 0)
        use(2 * j + 1, 1)
        return carry

    lax.fori_loop(0, (count - 1) // 2, body, 0)
    if count % 2 == 0:
        make(count - 1, 1)
        use(count - 2, 0)
        use(count - 1, 1)
    else:
        use(count - 1, 0)


def fill_table(table_ref, rows_ref):
    cols = table_ref.shape[1]
    for chunk in range(cols // LANES):
        lanes = slice(chunk * LANES, (chunk + 1) * LANES)
        for k, row in enumerate(table_rows(table_ref, lanes)):
            rows_ref[k * SUB : (k + 1) * SUB, lanes] = row


def decode_block(idx_ref, rows_ref, i, half, store):
    cols = idx_ref.shape[1]
    for chunk in range(cols // LANES):
        lanes = slice(chunk * LANES, (chunk + 1) * LANES)
        table = [rows_ref[k * SUB : (k + 1) * SUB, lanes] for k in range(16)]
        for step in range(half // SUB):
            row = pl.multiple_of(i * half + step * SUB, SUB)
            words = idx_ref[pl.ds(row, SUB), lanes].astype(jnp.int16)
            for parity in range(2):
                store(parity * half + step * SUB, lanes, look_up(table, bit_masks(words, parity)))


def up_kernel(x_ref, idx_ref, table_ref, pre_ref, weight_ref, rows_ref, *slots):
    count, _, block = x_ref.shape
    fill_table(table_ref, rows_ref)
    pre_ref[...] = jnp.zeros_like(pre_ref)

    def make(i, slot):
        def store(row, lanes, value):
            slots[slot][row : row + SUB, lanes] = value
            weight_ref[pl.ds(pl.multiple_of(i * block + row, SUB), SUB), lanes] = value

        decode_block(idx_ref, rows_ref, i, block // 2, store)

    def use(i, slot):
        pre_ref[...] += jnp.dot(x_ref[i], slots[slot][...], preferred_element_type=F32)

    pipelined(count, make, use)


def up_product(x_blocks, index, lookup):
    count, tokens, block = x_blocks.shape
    words, width = index.shape
    cols = divisor(width, 256)
    return pl.pallas_call(
        up_kernel,
        grid=(width // cols,),
        in_specs=[
            pl.BlockSpec((count, tokens, block), lambda j: (0, 0, 0)),
            pl.BlockSpec((words, cols), lambda j: (0, j)),
            pl.BlockSpec((16, cols), lambda j: (0, j)),
        ],
        out_specs=[
            pl.BlockSpec((tokens, cols), lambda j: (0, j)),
            pl.BlockSpec((2 * words, cols), lambda j: (0, j)),
        ],
        out_shape=[
            jax.ShapeDtypeStruct((tokens, width), F32),
            jax.ShapeDtypeStruct((2 * words, width), BF16),
        ],
        scratch_shapes=[pltpu.VMEM((16 * SUB, cols), BF16)] + [pltpu.VMEM((block, cols), BF16)] * 2,
        name="up_product",
    )(x_blocks, index, lookup)


def down_kernel(og_ref, idx_ref, table_ref, out_ref, rows_ref, *slots):
    count, _, block = out_ref.shape
    fill_table(table_ref, rows_ref)

    @pl.when(pl.program_id(0) == 0)
    def _():
        out_ref[...] = jnp.zeros_like(out_ref)

    def make(i, slot):
        def store(row, lanes, value):
            slots[slot][row : row + SUB, lanes] = value

        decode_block(idx_ref, rows_ref, i, block // 2, store)

    def use(i, slot):
        out_ref[i] += contract_cols(og_ref[...], slots[slot][...])

    pipelined(count, make, use)


def down_product(out_grad, index, lookup):
    tokens = out_grad.shape[0]
    words, width = index.shape
    cols = divisor(width, 256)
    block = math.gcd(2 * words, 256)
    count = 2 * words // block
    return pl.pallas_call(
        down_kernel,
        grid=(width // cols,),
        in_specs=[
            pl.BlockSpec((tokens, cols), lambda j: (0, j)),
            pl.BlockSpec((words, cols), lambda j: (0, j)),
            pl.BlockSpec((16, cols), lambda j: (0, j)),
        ],
        out_specs=pl.BlockSpec((count, tokens, block), lambda j: (0, 0, 0)),
        out_shape=jax.ShapeDtypeStruct((count, tokens, block), F32),
        scratch_shapes=[pltpu.VMEM((16 * SUB, cols), BF16)] + [pltpu.VMEM((block, cols), BF16)] * 2,
        name="down_product",
    )(out_grad, index, lookup)


def contract_cols(left, right):
    return lax.dot_general(left, right, (((1,), (1,)), ((), ())), preferred_element_type=F32)


def input_kernel(gate_ref, up_ref, wg_ref, wu_ref, out_ref):
    count, _, block = out_ref.shape

    @pl.when(pl.program_id(0) == 0)
    def _():
        out_ref[...] = jnp.zeros_like(out_ref)

    gate, up = gate_ref[...], up_ref[...]

    def body(i, carry):
        rows = pl.ds(pl.multiple_of(i * block, block), block)
        out_ref[i] += contract_cols(gate, wg_ref[rows, :]) + contract_cols(up, wu_ref[rows, :])
        return carry

    lax.fori_loop(0, count, body, 0, unroll=2 if count % 2 == 0 else 1)


def input_product(gate_grad, up_grad, w_gate, w_up):
    tokens, width = gate_grad.shape
    rows = w_gate.shape[0]
    cols = divisor(width, 256)
    block = math.gcd(rows, 256)
    grad = pl.BlockSpec((tokens, cols), lambda j: (0, j))
    weight = pl.BlockSpec((rows, cols), lambda j: (0, j))
    return pl.pallas_call(
        input_kernel,
        grid=(width // cols,),
        in_specs=[grad, grad, weight, weight],
        out_specs=pl.BlockSpec((rows // block, tokens, block), lambda j: (0, 0, 0)),
        out_shape=jax.ShapeDtypeStruct((rows // block, tokens, block), F32),
        name="input_product",
    )(gate_grad, up_grad, w_gate, w_up)


def leaves(value, masks):
    b0, b1, b2, b3 = masks
    zero = jnp.zeros_like(value)
    out = []
    for part in (jnp.where(b3, zero, value), jnp.where(b3, value, zero)):
        for piece in (jnp.where(b2, zero, part), jnp.where(b2, part, zero)):
            one = jnp.where(b1, piece, zero)
            out += [piece, jnp.where(b0, piece, zero), one, jnp.where(b0, one, zero)]
    return out


def write_bins(acc_ref, out_ref, scale):
    rows = [jnp.sum(acc_ref[8 * k : 8 * k + 8, :], axis=0, keepdims=True) for k in range(16)]
    for k in range(0, 16, 4):
        none, low, high, both = rows[k : k + 4]
        out_ref[k : k + 1, :] = ((none - low) - (high - both)) * scale
        out_ref[k + 1 : k + 2, :] = (low - both) * scale
        out_ref[k + 2 : k + 3, :] = (high - both) * scale
        out_ref[k + 3 : k + 4, :] = both * scale


def bins_kernel(scale, left_ref, right_ref, idx_ref, out_ref, acc_ref, *slots):
    count, block, _ = left_ref.shape
    half = block // 2
    cols = idx_ref.shape[1]
    acc_ref[...] = jnp.zeros_like(acc_ref)

    def make(i, slot):
        slots[slot][...] = jnp.dot(left_ref[i], right_ref[...], preferred_element_type=F32).astype(BF16)

    def use(i, slot):
        for chunk in range(cols // LANES):
            lanes = slice(chunk * LANES, (chunk + 1) * LANES)
            sums = None
            for step in range(half // SUB):
                row = pl.multiple_of(i * half + step * SUB, SUB)
                words = idx_ref[pl.ds(row, SUB), lanes].astype(jnp.int16)
                for parity in range(2):
                    first = parity * half + step * SUB
                    parts = leaves(slots[slot][first : first + SUB, lanes], bit_masks(words, parity))
                    sums = parts if sums is None else [a + b for a, b in zip(sums, parts)]
            for k, total in enumerate(sums):
                wide = total.astype(F32)
                acc_ref[8 * k : 8 * k + 8, lanes] += wide[:8] + wide[8:]

    pipelined(count, make, use)
    write_bins(acc_ref, out_ref, scale)


def bins(left_blocks, right, index, scale):
    count, tokens, block = left_blocks.shape
    words, width = index.shape
    cols = divisor(width, 256)
    return pl.pallas_call(
        functools.partial(bins_kernel, scale),
        grid=(width // cols,),
        in_specs=[
            pl.BlockSpec((count, block, tokens), lambda j: (0, 0, 0)),
            pl.BlockSpec((tokens, cols), lambda j: (0, j)),
            pl.BlockSpec((words, cols), lambda j: (0, j)),
        ],
        out_specs=pl.BlockSpec((16, cols), lambda j: (0, j)),
        out_shape=jax.ShapeDtypeStruct((16, width), F32),
        scratch_shapes=[pltpu.VMEM((128, cols), F32)] + [pltpu.VMEM((block, cols), BF16)] * 2,
        name="bins",
    )(jnp.swapaxes(left_blocks, 1, 2), right, index)


def pairing(block, dtype):
    row = jnp.arange(block)[:, None]
    col = jnp.arange(block)[None, :]
    half = block // 2
    return (row == 2 * (col % half) + col // half).astype(dtype)


def to_blocks(array):
    rows, cols = array.shape
    block = math.gcd(cols, 256)
    out = lax.dot_general(
        array.reshape(rows, cols // block, block), pairing(block, array.dtype), (((2,), (0,)), ((), ())),
        preferred_element_type=F32,
    )
    return jnp.swapaxes(out.astype(array.dtype), 0, 1)


def from_blocks(blocks):
    count, rows, block = blocks.shape
    out = lax.dot_general(
        blocks, pairing(block, blocks.dtype), (((2,), (1,)), ((), ())), precision=lax.Precision.HIGHEST,
        preferred_element_type=F32,
    )
    return jnp.swapaxes(out, 0, 1).reshape(rows, count * block)


def exchange(array, axis, size, bit):
    return lax.ppermute(array, axis, [(i, i ^ bit) for i in range(size)])


def axis_bits(size):
    return [1 << i for i in range(size.bit_length() - 1)]


def sum_scatter(array, axis):
    size = lax.axis_size(axis)
    if size & (size - 1):
        return lax.psum_scatter(array, axis, scatter_dimension=0, tiled=True)
    me = lax.axis_index(axis)
    rows, cols = array.shape
    array = array.reshape(size, rows // size, cols)
    for bit in axis_bits(size):
        pairs = array.reshape(array.shape[0] // 2, 2, rows // size, cols)
        mine = jnp.bitwise_and(me // bit, 1)
        sent = exchange(lax.dynamic_index_in_dim(pairs, 1 - mine, 1, False), axis, size, bit)
        array = lax.dynamic_index_in_dim(pairs, mine, 1, False) + sent
    return array.reshape(rows // size, cols)


def gather(array, axis):
    size = lax.axis_size(axis)
    if size & (size - 1):
        return lax.all_gather(array, axis, axis=0, tiled=True)
    me = lax.axis_index(axis)
    rows, cols = array.shape
    array = array[None]
    for bit in reversed(axis_bits(size)):
        other = exchange(array, axis, size, bit)
        first = jnp.bitwise_and(me // bit, 1) == 0
        low, high = jnp.where(first, array, other), jnp.where(first, other, array)
        array = jnp.stack([low, high], axis=1).reshape(-1, rows, cols)
    return array.reshape(size * rows, cols)


def sum_all(array, axis):
    size = lax.axis_size(axis)
    if size & (size - 1):
        return lax.psum(array, axis)
    for bit in axis_bits(size):
        array = array + exchange(array, axis, size, bit)
    return array


def after(array, *done):
    return lax.optimization_barrier((array, *done))[0]


def local_hidden(pre_gate, pre_up, hidden_grad):
    sig_gate = jax.nn.sigmoid(pre_gate)
    silu_gate = pre_gate * sig_gate
    activ = (silu_gate * pre_up).astype(BF16)
    gate_grad = (hidden_grad * pre_up * sig_gate * (1.0 + pre_gate * (1.0 - sig_gate))).astype(BF16)
    up_grad = (hidden_grad * silu_gate).astype(BF16)
    return activ, gate_grad, up_grad


def shards(inputs, out_grad, gate_index, up_index, down_index, gate_table, up_table, down_table):
    tokens = inputs.shape[0]
    width = gate_index.shape[1]
    scale = 1.0 / tokens
    hid_blocks = down_product(out_grad, down_index, down_table)
    count, _, block = hid_blocks.shape
    hid = lax.psum_scatter(hid_blocks, "inp", scatter_dimension=1, tiled=True)
    x_blocks = to_blocks(inputs)
    pre_gate, w_gate = up_product(x_blocks, gate_index, after(gate_table, hid_blocks))
    gate_share = lax.psum_scatter(pre_gate, "inp", scatter_dimension=0, tiled=True)
    pre_up, w_up = up_product(x_blocks, up_index, after(up_table, pre_gate))
    up_share = sum_scatter(pre_up, "inp")
    activ, gate_grad, up_grad = local_hidden(gate_share, up_share, from_blocks(hid))
    grads = gather(jnp.concatenate([gate_grad, up_grad], axis=1), "inp")
    gate_grad, up_grad = grads[:, :width], grads[:, width:]
    acts = gather(after(activ, gate_grad), "inp")
    din_blocks = input_product(gate_grad, up_grad, w_gate, w_up)
    din = lax.psum_scatter(din_blocks, "hid", scatter_dimension=1, tiled=True)
    input_grad = from_blocks(din).astype(BF16)
    act_blocks = to_blocks(after(acts, din_blocks))
    down_part = bins(act_blocks, out_grad, down_index, scale)
    down_sum = lax.psum(after(down_part, din), "hid")
    gate_part = bins(x_blocks, after(gate_grad, down_part, din), gate_index, scale)
    up_part = bins(x_blocks, after(up_grad, gate_part, down_sum), up_index, scale)
    up_width = up_part.shape[1]
    sums = sum_all(jnp.concatenate([gate_part, up_part], axis=1), "inp")
    gate_sum, up_sum = sums[:, :up_width], sums[:, up_width:]
    return input_grad, gate_sum, up_sum, down_sum


def solution(mesh):
    in_specs = (
        P(None, "inp"),
        P(None, "inp"),
        P("inp", "hid"),
        P("inp", "hid"),
        P("hid", "inp"),
        P(None, "hid"),
        P(None, "hid"),
        P(None, "inp"),
    )
    out_specs = (P("hid", "inp"), P(None, "hid"), P(None, "hid"), P(None, "inp"))
    return jax.shard_map(shards, mesh=mesh, in_specs=in_specs, out_specs=out_specs, check_vma=False)
```

```python
import functools
import math

import jax
import jax.numpy as jnp
from jax import lax
from jax.experimental import pallas as pl
from jax.experimental.pallas import tpu as pltpu
from jax.sharding import PartitionSpec as P

LANES = 128
SUB = 16
F32 = jnp.float32
BF16 = jnp.bfloat16


def divisor(size, most, unit=LANES):
    best = unit
    for cand in range(unit, most + 1, unit):
        if size % cand == 0:
            best = cand
    return best


def bit_masks(words, parity):
    return [(words & jnp.int16(1 << (4 * parity + bit))) != 0 for bit in range(4)]


def look_up(levels, masks):
    for mask in masks:
        levels = [jnp.where(mask, levels[i + 1], levels[i]) for i in range(0, len(levels), 2)]
    return levels[0]


def table_rows(table_ref, lanes):
    return [
        jnp.broadcast_to(table_ref[k : k + 1, lanes], (SUB, LANES)).astype(BF16)
        for k in range(16)
    ]


def pipelined(count, make, use):
    make(0, 0)

    def body(j, carry):
        make(2 * j + 1, 1)
        use(2 * j, 0)
        make(2 * j + 2, 0)
        use(2 * j + 1, 1)
        return carry

    lax.fori_loop(0, (count - 1) // 2, body, 0)
    if count % 2 == 0:
        make(count - 1, 1)
        use(count - 2, 0)
        use(count - 1, 1)
    else:
        use(count - 1, 0)


def decode_tile(idx_ref, table_ref, weight_ref, half):
    words, cols = idx_ref.shape
    for chunk in range(cols // LANES):
        lanes = slice(chunk * LANES, (chunk + 1) * LANES)
        table = table_rows(table_ref, lanes)

        def body(i, carry):
            for step in range(half // SUB):
                piece = idx_ref[pl.ds(pl.multiple_of(i * half + step * SUB, SUB), SUB), lanes].astype(jnp.int16)
                for parity in range(2):
                    row = pl.multiple_of((2 * i + parity) * half + step * SUB, SUB)
                    weight_ref[pl.ds(row, SUB), lanes] = look_up(table, bit_masks(piece, parity))
            return carry

        lax.fori_loop(0, words // half, body, 0)


def up_kernel(x_ref, idx_ref, table_ref, pre_ref, weight_ref):
    count, _, block = x_ref.shape
    decode_tile(idx_ref, table_ref, weight_ref, block // 2)
    pre_ref[...] = sum(
        jnp.dot(x_ref[i], weight_ref[i * block : (i + 1) * block, :], preferred_element_type=F32)
        for i in range(count)
    )


def up_product(x_blocks, index, lookup):
    count, tokens, block = x_blocks.shape
    words, width = index.shape
    cols = divisor(width, 256)
    return pl.pallas_call(
        up_kernel,
        grid=(width // cols,),
        in_specs=[
            pl.BlockSpec((count, tokens, block), lambda j: (0, 0, 0)),
            pl.BlockSpec((words, cols), lambda j: (0, j)),
            pl.BlockSpec((16, cols), lambda j: (0, j)),
        ],
        out_specs=[
            pl.BlockSpec((tokens, cols), lambda j: (0, j)),
            pl.BlockSpec((2 * words, cols), lambda j: (0, j)),
        ],
        out_shape=[
            jax.ShapeDtypeStruct((tokens, width), F32),
            jax.ShapeDtypeStruct((2 * words, width), BF16),
        ],
        name="up_product",
    )(x_blocks, index, lookup)


def down_kernel(og_ref, idx_ref, table_ref, out_ref, weight_ref):
    count, _, block = out_ref.shape

    @pl.when(pl.program_id(0) == 0)
    def _():
        out_ref[...] = jnp.zeros_like(out_ref)

    decode_tile(idx_ref, table_ref, weight_ref, block // 2)
    for i in range(count):
        out_ref[i] += contract_cols(og_ref[...], weight_ref[i * block : (i + 1) * block, :])


def down_product(out_grad, index, lookup):
    tokens = out_grad.shape[0]
    words, width = index.shape
    cols = divisor(width, 256)
    block = math.gcd(2 * words, 256)
    count = 2 * words // block
    return pl.pallas_call(
        down_kernel,
        grid=(width // cols,),
        in_specs=[
            pl.BlockSpec((tokens, cols), lambda j: (0, j)),
            pl.BlockSpec((words, cols), lambda j: (0, j)),
            pl.BlockSpec((16, cols), lambda j: (0, j)),
        ],
        out_specs=pl.BlockSpec((count, tokens, block), lambda j: (0, 0, 0)),
        out_shape=jax.ShapeDtypeStruct((count, tokens, block), F32),
        scratch_shapes=[pltpu.VMEM((2 * words, cols), BF16)],
        name="down_product",
    )(out_grad, index, lookup)


def contract_cols(left, right):
    return lax.dot_general(left, right, (((1,), (1,)), ((), ())), preferred_element_type=F32)


def input_kernel(gate_ref, up_ref, wg_ref, wu_ref, out_ref):
    count, _, block = out_ref.shape

    @pl.when(pl.program_id(0) == 0)
    def _():
        out_ref[...] = jnp.zeros_like(out_ref)

    gate, up = gate_ref[...], up_ref[...]

    def body(i, carry):
        rows = pl.ds(pl.multiple_of(i * block, block), block)
        out_ref[i] += contract_cols(gate, wg_ref[rows, :]) + contract_cols(up, wu_ref[rows, :])
        return carry

    lax.fori_loop(0, count, body, 0, unroll=2 if count % 2 == 0 else 1)


def input_product(gate_grad, up_grad, w_gate, w_up):
    tokens, width = gate_grad.shape
    rows = w_gate.shape[0]
    cols = divisor(width, 256)
    block = math.gcd(rows, 256)
    grad = pl.BlockSpec((tokens, cols), lambda j: (0, j))
    weight = pl.BlockSpec((rows, cols), lambda j: (0, j))
    return pl.pallas_call(
        input_kernel,
        grid=(width // cols,),
        in_specs=[grad, grad, weight, weight],
        out_specs=pl.BlockSpec((rows // block, tokens, block), lambda j: (0, 0, 0)),
        out_shape=jax.ShapeDtypeStruct((rows // block, tokens, block), F32),
        name="input_product",
    )(gate_grad, up_grad, w_gate, w_up)


def leaves(value, masks):
    b0, b1, b2, b3 = masks
    zero = jnp.zeros_like(value)
    out = []
    for part in (jnp.where(b3, zero, value), jnp.where(b3, value, zero)):
        for piece in (jnp.where(b2, zero, part), jnp.where(b2, part, zero)):
            one = jnp.where(b1, piece, zero)
            out += [piece, jnp.where(b0, piece, zero), one, jnp.where(b0, one, zero)]
    return out


def write_bins(acc_ref, out_ref, scale):
    rows = [jnp.sum(acc_ref[8 * k : 8 * k + 8, :], axis=0, keepdims=True) for k in range(16)]
    for k in range(0, 16, 4):
        none, low, high, both = rows[k : k + 4]
        out_ref[k : k + 1, :] = ((none - low) - (high - both)) * scale
        out_ref[k + 1 : k + 2, :] = (low - both) * scale
        out_ref[k + 2 : k + 3, :] = (high - both) * scale
        out_ref[k + 3 : k + 4, :] = both * scale


def bins_kernel(scale, left_ref, right_ref, idx_ref, out_ref, acc_ref, *slots):
    count, block, _ = left_ref.shape
    half = block // 2
    cols = idx_ref.shape[1]
    acc_ref[...] = jnp.zeros_like(acc_ref)

    def make(i, slot):
        slots[slot][...] = jnp.dot(left_ref[i], right_ref[...], preferred_element_type=F32).astype(BF16)

    def use(i, slot):
        for chunk in range(cols // LANES):
            lanes = slice(chunk * LANES, (chunk + 1) * LANES)
            sums = None
            for step in range(half // SUB):
                row = pl.multiple_of(i * half + step * SUB, SUB)
                words = idx_ref[pl.ds(row, SUB), lanes].astype(jnp.int16)
                for parity in range(2):
                    first = parity * half + step * SUB
                    parts = leaves(slots[slot][first : first + SUB, lanes], bit_masks(words, parity))
                    sums = parts if sums is None else [a + b for a, b in zip(sums, parts)]
            for k, total in enumerate(sums):
                wide = total.astype(F32)
                acc_ref[8 * k : 8 * k + 8, lanes] += wide[:8] + wide[8:]

    pipelined(count, make, use)
    write_bins(acc_ref, out_ref, scale)


def bins(left_blocks, right, index, scale):
    count, tokens, block = left_blocks.shape
    words, width = index.shape
    cols = divisor(width, 256)
    return pl.pallas_call(
        functools.partial(bins_kernel, scale),
        grid=(width // cols,),
        in_specs=[
            pl.BlockSpec((count, block, tokens), lambda j: (0, 0, 0)),
            pl.BlockSpec((tokens, cols), lambda j: (0, j)),
            pl.BlockSpec((words, cols), lambda j: (0, j)),
        ],
        out_specs=pl.BlockSpec((16, cols), lambda j: (0, j)),
        out_shape=jax.ShapeDtypeStruct((16, width), F32),
        scratch_shapes=[pltpu.VMEM((128, cols), F32)] + [pltpu.VMEM((block, cols), BF16)] * 2,
        name="bins",
    )(jnp.swapaxes(left_blocks, 1, 2), right, index)


def pairing(block, dtype):
    row = jnp.arange(block)[:, None]
    col = jnp.arange(block)[None, :]
    half = block // 2
    return (row == 2 * (col % half) + col // half).astype(dtype)


def to_blocks(array):
    rows, cols = array.shape
    block = math.gcd(cols, 256)
    out = lax.dot_general(
        array.reshape(rows, cols // block, block), pairing(block, array.dtype), (((2,), (0,)), ((), ())),
        preferred_element_type=F32,
    )
    return jnp.swapaxes(out.astype(array.dtype), 0, 1)


def from_blocks(blocks):
    count, rows, block = blocks.shape
    out = lax.dot_general(
        blocks, pairing(block, blocks.dtype), (((2,), (1,)), ((), ())), precision=lax.Precision.HIGHEST,
        preferred_element_type=F32,
    )
    return jnp.swapaxes(out, 0, 1).reshape(rows, count * block)


def exchange(array, axis, size, bit):
    return lax.ppermute(array, axis, [(i, i ^ bit) for i in range(size)])


def axis_bits(size):
    return [1 << i for i in range(size.bit_length() - 1)]


def sum_scatter(array, axis):
    size = lax.axis_size(axis)
    if size & (size - 1):
        return lax.psum_scatter(array, axis, scatter_dimension=0, tiled=True)
    me = lax.axis_index(axis)
    rows, cols = array.shape
    array = array.reshape(size, rows // size, cols)
    for bit in axis_bits(size):
        pairs = array.reshape(array.shape[0] // 2, 2, rows // size, cols)
        mine = jnp.bitwise_and(me // bit, 1)
        sent = exchange(lax.dynamic_index_in_dim(pairs, 1 - mine, 1, False), axis, size, bit)
        array = lax.dynamic_index_in_dim(pairs, mine, 1, False) + sent
    return array.reshape(rows // size, cols)


def gather(array, axis):
    size = lax.axis_size(axis)
    if size & (size - 1):
        return lax.all_gather(array, axis, axis=0, tiled=True)
    me = lax.axis_index(axis)
    rows, cols = array.shape
    array = array[None]
    for bit in reversed(axis_bits(size)):
        other = exchange(array, axis, size, bit)
        first = jnp.bitwise_and(me // bit, 1) == 0
        low, high = jnp.where(first, array, other), jnp.where(first, other, array)
        array = jnp.stack([low, high], axis=1).reshape(-1, rows, cols)
    return array.reshape(size * rows, cols)


def sum_all(array, axis):
    size = lax.axis_size(axis)
    if size & (size - 1):
        return lax.psum(array, axis)
    for bit in axis_bits(size):
        array = array + exchange(array, axis, size, bit)
    return array


def after(array, *done):
    return lax.optimization_barrier((array, *done))[0]


def local_hidden(pre_gate, pre_up, hidden_grad):
    sig_gate = jax.nn.sigmoid(pre_gate)
    silu_gate = pre_gate * sig_gate
    activ = (silu_gate * pre_up).astype(BF16)
    gate_grad = (hidden_grad * pre_up * sig_gate * (1.0 + pre_gate * (1.0 - sig_gate))).astype(BF16)
    up_grad = (hidden_grad * silu_gate).astype(BF16)
    return activ, gate_grad, up_grad


def shards(inputs, out_grad, gate_index, up_index, down_index, gate_table, up_table, down_table):
    tokens = inputs.shape[0]
    width = gate_index.shape[1]
    scale = 1.0 / tokens
    hid_blocks = down_product(out_grad, down_index, down_table)
    count, _, block = hid_blocks.shape
    hid = lax.psum_scatter(hid_blocks, "inp", scatter_dimension=1, tiled=True)
    x_blocks = to_blocks(inputs)
    pre_gate, w_gate = up_product(x_blocks, gate_index, after(gate_table, hid_blocks))
    gate_share = lax.psum_scatter(pre_gate, "inp", scatter_dimension=0, tiled=True)
    pre_up, w_up = up_product(x_blocks, up_index, after(up_table, pre_gate))
    up_share = sum_scatter(pre_up, "inp")
    activ, gate_grad, up_grad = local_hidden(gate_share, up_share, from_blocks(hid))
    grads = gather(jnp.concatenate([gate_grad, up_grad], axis=1), "inp")
    gate_grad, up_grad = grads[:, :width], grads[:, width:]
    acts = gather(after(activ, gate_grad), "inp")
    din_blocks = input_product(gate_grad, up_grad, w_gate, w_up)
    din = lax.psum_scatter(din_blocks, "hid", scatter_dimension=1, tiled=True)
    input_grad = from_blocks(din).astype(BF16)
    act_blocks = to_blocks(after(acts, din_blocks))
    down_part = bins(act_blocks, out_grad, down_index, scale)
    down_sum = lax.psum(after(down_part, din), "hid")
    gate_part = bins(x_blocks, after(gate_grad, down_part, din), gate_index, scale)
    up_part = bins(x_blocks, after(up_grad, gate_part, down_sum), up_index, scale)
    up_width = up_part.shape[1]
    sums = sum_all(jnp.concatenate([gate_part, up_part], axis=1), "inp")
    gate_sum, up_sum = sums[:, :up_width], sums[:, up_width:]
    return input_grad, gate_sum, up_sum, down_sum


def solution(mesh):
    in_specs = (
        P(None, "inp"),
        P(None, "inp"),
        P("inp", "hid"),
        P("inp", "hid"),
        P("hid", "inp"),
        P(None, "hid"),
        P(None, "hid"),
        P(None, "inp"),
    )
    out_specs = (P("hid", "inp"), P(None, "hid"), P(None, "hid"), P(None, "inp"))
    return jax.shard_map(shards, mesh=mesh, in_specs=in_specs, out_specs=out_specs, check_vma=False)
```
